32 devices in a mesh: tp: 4 (over y, core), fsdp: 8 (over z, x).
Axes of the slice: x: 2, y: 2, z: 4, core: 2. Of those that a mesh axis runs over, the one named last changes fastest.
Arguments:
- momentum: float32 [8192, 28672], P('tp', 'fsdp'), may hold values from -6 to 6
- gradient: bfloat16 [8192, 28672], P('tp', 'fsdp'), may hold values from -6 to 6
- basis: float32 [28672, 512], P('fsdp', 'tp'), may hold values from -1 to 1
Outputs:
- new_momentum: float32 [8192, 28672], P('tp', 'fsdp')
- new_basis: float32 [28672, 512], P('fsdp', 'tp')
- left_factor: float32 [8192, 512], P(('tp', 'fsdp'))
The draws below stay inside these ranges and needn't reach their ends.
All inputs are finite; a program needn't handle non-finite values.
Results may differ from the reference program's by a relative error of at most 0.0003.
Values sent between devices are 32-bit elements; how exact they have to be, the bound alone decides.
A program may use at most 192 MiB of HBM per device.

```python
import math
import jax
import jax.numpy as jnp
from jax import lax

D = 8192
FF = 28672
RANK = 512


def draw_basis(key, part):
    first_key, second_key, third_key = jax.random.split(jax.random.fold_in(key, 7301), 3)
    half_rank = RANK // 2
    leading = jax.random.uniform(first_key, (FF, half_rank), jnp.float32, -1.0, 1.0)
    fresh_noise = jax.random.uniform(second_key, (FF, half_rank), jnp.float32, -1.0, 1.0)
    mixing = jnp.exp(jax.random.uniform(third_key, (1, half_rank), jnp.float32, math.log(0.004), math.log(0.008)))
    partner = (1.0 - mixing) * leading + mixing * fresh_noise
    return jnp.stack([leading, partner], axis=2).reshape(FF, RANK).astype(jnp.float32)


def shard_levels(stream_key, shape, shards, least, largest):
    factor_of, own = 1.0, jax.random.fold_in(stream_key, 6)
    for position, shards_of in shards:
        draws = jnp.exp(jax.random.uniform(jax.random.fold_in(own, position), (shards_of,), jnp.float32, least / len(shards), largest / len(shards)))
        factor_of = factor_of * jnp.repeat(draws, shape[position] // shards_of).reshape([-1 if axis == position else 1 for axis in range(len(shape))])
    return factor_of


def bell_draw(rng, dims, deviation, most, pieces=(), kind=jnp.bfloat16):
    array = jax.random.normal(rng, dims, jnp.float32) * deviation
    if len(pieces) > 0:
        array = shard_levels(rng, dims, pieces, -0.22, 0.18) * array
    return jnp.clip(array, min=-most, max=most).astype(kind)


def setup_inputs(seed: int = 0) -> dict:
    key_list = jax.random.split(jax.random.key(seed), 4)
    return {
        "momentum": bell_draw(key_list[0], (D, FF), 1.0, 6.0, ((0, 4), (1, 8)), jnp.float32),
        "gradient": bell_draw(key_list[1], (D, FF), 1.0, 6.0, ((0, 4), (1, 8))),
        "basis": draw_basis(jax.random.fold_in(key_list[3], 71), 0),
    }


keep_rate = 0.95
tiny = 1e-06
high = lax.Precision.HIGHEST

def orthonormal(left):
    for turn in range(2):
        gram = jnp.dot(left.T.astype(jnp.float32), left.astype(jnp.float32), precision=high, preferred_element_type=jnp.float32)
        lower = jnp.linalg.cholesky(gram)
        left = jax.scipy.linalg.solve_triangular(lower, left.T, lower=True).T
    return left

def reference(momentum, gradient, basis):
    blended = momentum + gradient.astype(jnp.float32)
    sketch = jnp.dot(blended.astype(jnp.float32), basis.astype(jnp.float32), precision=high, preferred_element_type=jnp.float32)
    left_factor = orthonormal(sketch)
    right = jnp.dot(blended.T.astype(jnp.float32), left_factor.astype(jnp.float32), precision=high, preferred_element_type=jnp.float32)
    new_momentum = blended - (1.0 - keep_rate) * jnp.dot(left_factor.astype(jnp.float32), right.T.astype(jnp.float32), precision=high, preferred_element_type=jnp.float32)
    scales = jnp.sqrt(lax.optimization_barrier(jnp.sum(right * right, axis=0)) + tiny)
    new_basis = right / scales[None, :]
    return (new_momentum, new_basis, left_factor)
```

```python
import functools

import jax
import jax.numpy as jnp
from jax import lax
from jax.experimental import pallas as pl
from jax.experimental.pallas import tpu as pltpu
from jax.sharding import PartitionSpec as P

keep_rate = 0.95
tiny = 1e-06
highest = lax.Precision.HIGHEST
BLOCK = 128
PANEL = 8


def product(a, b, dims, precision=highest):
    return lax.dot_general(a, b, ((dims[:1], dims[1:]), ((), ())), precision=precision, preferred_element_type=jnp.float32)


def eliminate_block(m_ref):
    lanes = lax.broadcasted_iota(jnp.int32, (PANEL, BLOCK), 1)
    subs = lax.broadcasted_iota(jnp.int32, (PANEL, BLOCK), 0)
    rows = lax.broadcasted_iota(jnp.int32, (BLOCK, BLOCK), 0)
    columns = lax.broadcasted_iota(jnp.int32, (BLOCK, BLOCK), 1)
    for start in range(0, BLOCK, PANEL):
        panel = m_ref[start:start + PANEL, :]
        heads = [jnp.broadcast_to(panel[:, start + j:start + j + 1], (PANEL, BLOCK)) for j in range(PANEL)]
        for j in range(PANEL):
            head = heads[j]
            pivot = jnp.broadcast_to(head[j:j + 1, :], (PANEL, BLOCK))
            root = lax.rsqrt(pivot)
            root = root * (1.5 - 0.5 * (pivot * root) * root)
            factor = jnp.where(subs > j, head * root, 0.0)
            row = jnp.broadcast_to(panel[j:j + 1, :], (PANEL, BLOCK)) * root
            row = jnp.where(lanes == start + j, root, row)
            kept = jnp.where((lanes == start + j) & (subs > j), 0.0, panel)
            panel = jnp.where(subs == j, row, kept - factor * row)
            for later in range(j + 1, PANEL):
                scaled = jnp.broadcast_to(heads[later][j:j + 1, :], (PANEL, BLOCK)) * root
                heads[later] = heads[later] - factor * scaled
        m_ref[start:start + PANEL, :] = jnp.where(lanes > start + subs, 0.0, panel)
        stop = start + PANEL
        if stop < BLOCK:
            right = jnp.where(lanes >= stop, panel, 0.0)
            own = jnp.where((lanes > start + subs) & (lanes < stop), 0.0, panel)
            update = product(right, own, (0, 0))
            below = m_ref[stop:, :]
            fresh = (columns[stop:] >= start) & (columns[stop:] < stop)
            m_ref[stop:, :] = jnp.where(fresh, 0.0, below) - update[stop:, :]


def inverse_factor_kernel(g_ref, x_ref, m_ref):
    n = g_ref.shape[0]
    x_ref[...] = g_ref[...]
    for start in range(0, n, BLOCK):
        stop = start + BLOCK
        m_ref[...] = x_ref[start:stop, start:stop]
        eliminate_block(m_ref)
        diagonal = m_ref[...]
        x_ref[start:stop, start:stop] = diagonal
        if start > 0:
            x_ref[start:stop, :start] = product(diagonal, x_ref[start:stop, :start], (1, 0))
        if stop < n:
            right = product(diagonal, x_ref[start:stop, stop:], (1, 0))
            if start > 0:
                x_ref[stop:, :start] -= product(right, x_ref[start:stop, :start], (0, 0))
            x_ref[stop:, start:stop] = -product(right, diagonal, (0, 0))
            x_ref[stop:, stop:] -= product(right, right, (0, 0))
            x_ref[start:stop, stop:] = jnp.zeros((BLOCK, n - stop), jnp.float32)


def inverse_factor(gram):
    n = gram.shape[0]
    return pl.pallas_call(
        inverse_factor_kernel,
        out_shape=jax.ShapeDtypeStruct((n, n), jnp.float32),
        in_specs=[pl.BlockSpec(memory_space=pltpu.VMEM)],
        out_specs=pl.BlockSpec(memory_space=pltpu.VMEM),
        scratch_shapes=[pltpu.VMEM((BLOCK, BLOCK), jnp.float32)],
        cost_estimate=pl.CostEstimate(flops=2 * n * n * n * 20, bytes_accessed=8 * n * n, transcendentals=n),
        name="inverse_factor",
    )(gram)


MESH = pl.DeviceIdType.MESH


def sum_kernel(axes, sizes, g_ref, out_ref, land0, land1, sum0, sum1, send0, recv0, send1, recv1, send2, recv2, send3, recv3):
    (outer, inner), (count0, count1) = axes, sizes
    me0, me1 = lax.axis_index(outer), lax.axis_index(inner)
    rows0 = g_ref.shape[0] // count0
    rows1 = rows0 // count1

    def peer(axis, me, count, step):
        return {axis: lax.rem(me + step, count)}

    barrier = pltpu.get_barrier_semaphore()
    for axis, me, count in ((outer, me0, count0), (inner, me1, count1)):
        for step in range(1, count):
            pl.semaphore_signal(barrier, inc=1, device_id=peer(axis, me, count, step), device_id_type=MESH)
    pl.semaphore_wait(barrier, count0 + count1 - 2)

    def rows(index, size):
        return pl.ds(pl.multiple_of(index * size, size), size)

    def scatter(axis, me, count, size, source, land, send, recv):
        copies = []
        for step in range(1, count):
            target = lax.rem(me + step, count)
            copies.append(pltpu.make_async_remote_copy(
                src_ref=source.at[rows(target, size)], dst_ref=land.at[step], send_sem=send.at[step],
                recv_sem=recv.at[step], device_id={axis: target}, device_id_type=MESH))
        for copy in copies:
            copy.start()
        return copies

    def gather(axis, me, count, size, source, base, send, recv):
        copies = []
        for step in range(1, count):
            target = lax.rem(me + step, count)
            copies.append(pltpu.make_async_remote_copy(
                src_ref=source, dst_ref=out_ref.at[pl.ds(pl.multiple_of(base, size), size)], send_sem=send.at[step],
                recv_sem=recv.at[step], device_id={axis: target}, device_id_type=MESH))
        for copy in copies:
            copy.start()
        return copies

    first = scatter(outer, me0, count0, rows0, g_ref, land0, send0, recv0)
    total = g_ref[rows(me0, rows0), :]
    for step in range(1, count0):
        first[step - 1].wait_recv()
        total = total + land0[step]
    sum0[...] = total
    second = scatter(inner, me1, count1, rows1, sum0, land1, send1, recv1)
    total = sum0[rows(me1, rows1), :]
    for step in range(1, count1):
        second[step - 1].wait_recv()
        total = total + land1[step]
    sum1[...] = total
    place = me0 * rows0 + me1 * rows1
    third = gather(inner, me1, count1, rows1, sum1, place, send2, recv2)
    out_ref[pl.ds(pl.multiple_of(place, rows1), rows1), :] = total
    for copy in third:
        copy.wait_recv()
    base = me0 * rows0
    fourth = gather(outer, me0, count0, rows0, out_ref.at[rows(me0, rows0)], base, send3, recv3)
    for copy in fourth:
        copy.wait_recv()
    for copy in first + second + third + fourth:
        copy.wait_send()


def sum_over_devices(gram, axes):
    n, columns = gram.shape
    sizes = tuple(lax.axis_size(axis) for axis in axes)
    if max(sizes) > 8 or n % (8 * sizes[0] * sizes[1]):
        return lax.psum(gram, axes)
    rows0 = n // sizes[0]
    rows1 = rows0 // sizes[1]
    semaphores = [pltpu.SemaphoreType.DMA((size,)) for size in (sizes[0], sizes[0], sizes[1], sizes[1], sizes[1], sizes[1], sizes[0], sizes[0])]
    return pl.pallas_call(
        functools.partial(sum_kernel, axes, sizes),
        out_shape=jax.ShapeDtypeStruct((n, columns), jnp.float32),
        in_specs=[pl.BlockSpec(memory_space=pltpu.VMEM)],
        out_specs=pl.BlockSpec(memory_space=pltpu.VMEM),
        scratch_shapes=[
            pltpu.VMEM((sizes[0], rows0, columns), jnp.float32),
            pltpu.VMEM((sizes[1], rows1, columns), jnp.float32),
            pltpu.VMEM((rows0, columns), jnp.float32),
            pltpu.VMEM((rows1, columns), jnp.float32),
        ] + semaphores,
        compiler_params=pltpu.CompilerParams(collective_id=0, has_side_effects=True),
        cost_estimate=pl.CostEstimate(flops=n * columns * 2, bytes_accessed=8 * n * columns, transcendentals=0),
        name="sum_over_devices",
    )(gram)


def on_device(momentum, gradient, basis):
    tile = momentum + gradient.astype(jnp.float32)
    partial_sketch = product(tile, lax.all_gather(basis, "tp", axis=1, tiled=True), (1, 0))
    own = lax.psum_scatter(partial_sketch, "fsdp", scatter_dimension=0, tiled=True)
    gram = sum_over_devices(product(own, own, (0, 0)), ("fsdp", "tp"))
    half = own.shape[0] // 2
    gram, own_later = lax.optimization_barrier((gram, own[:half]))
    sketch = lax.all_gather(own_later, "fsdp", axis=0)
    inverse = inverse_factor(gram)
    own_first = product(own, inverse, (1, 1))
    gram = sum_over_devices(product(own_first, own_first, (0, 0)), ("fsdp", "tp"))
    gram, first_later = lax.optimization_barrier((gram, own_first[half:]))
    later_half = lax.all_gather(first_later, "fsdp", axis=0)
    second = inverse_factor(gram)
    own_left = product(own_first, second, (1, 1))
    early_half = lax.dot_general(sketch, inverse, (((2,), (1,)), ((), ())), precision=highest, preferred_element_type=jnp.float32)
    first = jnp.concatenate([early_half, later_half], axis=1).reshape(tile.shape[0], -1)
    left = product(first, second, (1, 1))
    partial_right = product(tile, left, (0, 0), lax.Precision.HIGH)
    mine = lax.psum_scatter(partial_right, "tp", scatter_dimension=1, tiled=True)
    squares = lax.psum(jnp.sum(mine * mine, axis=0), "fsdp")
    new_basis = mine / jnp.sqrt(squares + tiny)[None, :]
    full_right = lax.all_gather(mine, "tp", axis=1, tiled=True)
    new_momentum = tile - (1.0 - keep_rate) * product(left, full_right, (1, 1), lax.Precision.DEFAULT)
    return (new_momentum, new_basis, own_left)


def solution(mesh):
    placed = (P("tp", "fsdp"), P("tp", "fsdp"), P("fsdp", "tp"))
    return jax.shard_map(
        on_device,
        mesh=mesh,
        in_specs=placed,
        out_specs=(P("tp", "fsdp"), P("fsdp", "tp"), P(("tp", "fsdp"), None)),
        check_vma=False,
    )
```

```python
import functools

import jax
import jax.numpy as jnp
from jax import lax
from jax.experimental import pallas as pl
from jax.experimental.pallas import tpu as pltpu
from jax.sharding import PartitionSpec as P

keep_rate = 0.95
tiny = 1e-06
highest = lax.Precision.HIGHEST
BLOCK = 128
PANEL = 8


def product(a, b, dims, precision=highest):
    return lax.dot_general(a, b, ((dims[:1], dims[1:]), ((), ())), precision=precision, preferred_element_type=jnp.float32)


def eliminate_block(m_ref):
    lanes = lax.broadcasted_iota(jnp.int32, (PANEL, BLOCK), 1)
    subs = lax.broadcasted_iota(jnp.int32, (PANEL, BLOCK), 0)
    rows = lax.broadcasted_iota(jnp.int32, (BLOCK, BLOCK), 0)
    columns = lax.broadcasted_iota(jnp.int32, (BLOCK, BLOCK), 1)
    for start in range(0, BLOCK, PANEL):
        panel = m_ref[start:start + PANEL, :]
        heads = [jnp.broadcast_to(panel[:, start + j:start + j + 1], (PANEL, BLOCK)) for j in range(PANEL)]
        for j in range(PANEL):
            head = heads[j]
            pivot = jnp.broadcast_to(head[j:j + 1, :], (PANEL, BLOCK))
            root = lax.rsqrt(pivot)
            root = root * (1.5 - 0.5 * (pivot * root) * root)
            factor = jnp.where(subs > j, head * root, 0.0)
            row = jnp.broadcast_to(panel[j:j + 1, :], (PANEL, BLOCK)) * root
            row = jnp.where(lanes == start + j, root, row)
            kept = jnp.where((lanes == start + j) & (subs > j), 0.0, panel)
            panel = jnp.where(subs == j, row, kept - factor * row)
            for later in range(j + 1, PANEL):
                scaled = jnp.broadcast_to(heads[later][j:j + 1, :], (PANEL, BLOCK)) * root
                heads[later] = heads[later] - factor * scaled
        m_ref[start:start + PANEL, :] = jnp.where(lanes > start + subs, 0.0, panel)
        stop = start + PANEL
        if stop < BLOCK:
            right = jnp.where(lanes >= stop, panel, 0.0)
            own = jnp.where((lanes > start + subs) & (lanes < stop), 0.0, panel)
            update = product(right, own, (0, 0))
            below = m_ref[stop:, :]
            fresh = (columns[stop:] >= start) & (columns[stop:] < stop)
            m_ref[stop:, :] = jnp.where(fresh, 0.0, below) - update[stop:, :]


def inverse_factor_kernel(g_ref, x_ref, m_ref):
    n = g_ref.shape[0]
    x_ref[...] = g_ref[...]
    for start in range(0, n, BLOCK):
        stop = start + BLOCK
        m_ref[...] = x_ref[start:stop, start:stop]
        eliminate_block(m_ref)
        diagonal = m_ref[...]
        x_ref[start:stop, start:stop] = diagonal
        if start > 0:
            x_ref[start:stop, :start] = product(diagonal, x_ref[start:stop, :start], (1, 0))
        if stop < n:
            right = product(diagonal, x_ref[start:stop, stop:], (1, 0))
            if start > 0:
                x_ref[stop:, :start] -= product(right, x_ref[start:stop, :start], (0, 0))
            x_ref[stop:, start:stop] = -product(right, diagonal, (0, 0))
            x_ref[stop:, stop:] -= product(right, right, (0, 0))
            x_ref[start:stop, stop:] = jnp.zeros((BLOCK, n - stop), jnp.float32)


def inverse_factor(gram):
    n = gram.shape[0]
    return pl.pallas_call(
        inverse_factor_kernel,
        out_shape=jax.ShapeDtypeStruct((n, n), jnp.float32),
        in_specs=[pl.BlockSpec(memory_space=pltpu.VMEM)],
        out_specs=pl.BlockSpec(memory_space=pltpu.VMEM),
        scratch_shapes=[pltpu.VMEM((BLOCK, BLOCK), jnp.float32)],
        cost_estimate=pl.CostEstimate(flops=2 * n * n * n * 20, bytes_accessed=8 * n * n, transcendentals=n),
        name="inverse_factor",
    )(gram)


MESH = pl.DeviceIdType.MESH


def sum_kernel(axes, sizes, g_ref, out_ref, land0, land1, sum0, sum1, send0, recv0, send1, recv1, send2, recv2, send3, recv3):
    (outer, inner), (count0, count1) = axes, sizes
    me0, me1 = lax.axis_index(outer), lax.axis_index(inner)
    rows0 = g_ref.shape[0] // count0
    rows1 = rows0 // count1

    def peer(axis, me, count, step):
        return {axis: lax.rem(me + step, count)}

    barrier = pltpu.get_barrier_semaphore()
    for axis, me, count in ((outer, me0, count0), (inner, me1, count1)):
        for step in range(1, count):
            pl.semaphore_signal(barrier, inc=1, device_id=peer(axis, me, count, step), device_id_type=MESH)
    pl.semaphore_wait(barrier, count0 + count1 - 2)

    def rows(index, size):
        return pl.ds(pl.multiple_of(index * size, size), size)

    def scatter(axis, me, count, size, source, land, send, recv):
        copies = []
        for step in range(1, count):
            target = lax.rem(me + step, count)
            copies.append(pltpu.make_async_remote_copy(
                src_ref=source.at[rows(target, size)], dst_ref=land.at[step], send_sem=send.at[step],
                recv_sem=recv.at[step], device_id={axis: target}, device_id_type=MESH))
        for copy in copies:
            copy.start()
        return copies

    def gather(axis, me, count, size, source, base, send, recv):
        copies = []
        for step in range(1, count):
            target = lax.rem(me + step, count)
            copies.append(pltpu.make_async_remote_copy(
                src_ref=source, dst_ref=out_ref.at[pl.ds(pl.multiple_of(base, size), size)], send_sem=send.at[step],
                recv_sem=recv.at[step], device_id={axis: target}, device_id_type=MESH))
        for copy in copies:
            copy.start()
        return copies

    first = scatter(outer, me0, count0, rows0, g_ref, land0, send0, recv0)
    total = g_ref[rows(me0, rows0), :]
    for step in range(1, count0):
        first[step - 1].wait_recv()
        total = total + land0[step]
    sum0[...] = total
    second = scatter(inner, me1, count1, rows1, sum0, land1, send1, recv1)
    total = sum0[rows(me1, rows1), :]
    for step in range(1, count1):
        second[step - 1].wait_recv()
        total = total + land1[step]
    sum1[...] = total
    place = me0 * rows0 + me1 * rows1
    third = gather(inner, me1, count1, rows1, sum1, place, send2, recv2)
    out_ref[pl.ds(pl.multiple_of(place, rows1), rows1), :] = total
    for copy in third:
        copy.wait_recv()
    base = me0 * rows0
    fourth = gather(outer, me0, count0, rows0, out_ref.at[rows(me0, rows0)], base, send3, recv3)
    for copy in fourth:
        copy.wait_recv()
    for copy in first + second + third + fourth:
        copy.wait_send()


def sum_over_devices(gram, axes):
    n, columns = gram.shape
    sizes = tuple(lax.axis_size(axis) for axis in axes)
    if max(sizes) > 8 or n % (8 * sizes[0] * sizes[1]):
        return lax.psum(gram, axes)
    rows0 = n // sizes[0]
    rows1 = rows0 // sizes[1]
    semaphores = [pltpu.SemaphoreType.DMA((size,)) for size in (sizes[0], sizes[0], sizes[1], sizes[1], sizes[1], sizes[1], sizes[0], sizes[0])]
    return pl.pallas_call(
        functools.partial(sum_kernel, axes, sizes),
        out_shape=jax.ShapeDtypeStruct((n, columns), jnp.float32),
        in_specs=[pl.BlockSpec(memory_space=pltpu.VMEM)],
        out_specs=pl.BlockSpec(memory_space=pltpu.VMEM),
        scratch_shapes=[
            pltpu.VMEM((sizes[0], rows0, columns), jnp.float32),
            pltpu.VMEM((sizes[1], rows1, columns), jnp.float32),
            pltpu.VMEM((rows0, columns), jnp.float32),
            pltpu.VMEM((rows1, columns), jnp.float32),
        ] + semaphores,
        compiler_params=pltpu.CompilerParams(collective_id=0, has_side_effects=True),
        cost_estimate=pl.CostEstimate(flops=n * columns * 2, bytes_accessed=8 * n * columns, transcendentals=0),
        name="sum_over_devices",
    )(gram)


def on_device(momentum, gradient, basis):
    tile = momentum + gradient.astype(jnp.float32)
    depth = tile.shape[1] // 2
    early = lax.all_gather(basis[:depth], "tp", axis=1, tiled=True)
    late = lax.all_gather(basis[depth:], "tp", axis=1, tiled=True)
    partial_sketch = product(tile[:, :depth], early, (1, 0)) + product(tile[:, depth:], late, (1, 0))
    own = lax.psum_scatter(partial_sketch, "fsdp", scatter_dimension=0, tiled=True)
    gram = sum_over_devices(product(own, own, (0, 0)), ("fsdp", "tp"))
    half = own.shape[0] // 2
    gram, own_later = lax.optimization_barrier((gram, own[:half]))
    sketch = lax.all_gather(own_later, "fsdp", axis=0)
    inverse = inverse_factor(gram)
    own_first = product(own, inverse, (1, 1))
    gram = sum_over_devices(product(own_first, own_first, (0, 0)), ("fsdp", "tp"))
    gram, first_later = lax.optimization_barrier((gram, own_first[half:]))
    later_half = lax.all_gather(first_later, "fsdp", axis=0)
    second = inverse_factor(gram)
    own_left = product(own_first, second, (1, 1))
    early_half = lax.dot_general(sketch, inverse, (((2,), (1,)), ((), ())), precision=highest, preferred_element_type=jnp.float32)
    first = jnp.concatenate([early_half, later_half], axis=1).reshape(tile.shape[0], -1)
    left = product(first, second, (1, 1))
    partial_right = product(tile, left, (0, 0), lax.Precision.HIGH)
    mine = lax.psum_scatter(partial_right, "tp", scatter_dimension=1, tiled=True)
    squares = lax.psum(jnp.sum(mine * mine, axis=0), "fsdp")
    new_basis = mine / jnp.sqrt(squares + tiny)[None, :]
    full_right = lax.all_gather(mine, "tp", axis=1, tiled=True)
    new_momentum = tile - product(left, (1.0 - keep_rate) * full_right, (1, 1), lax.Precision.DEFAULT)
    return (new_momentum, new_basis, own_left)


def solution(mesh):
    placed = (P("tp", "fsdp"), P("tp", "fsdp"), P("fsdp", "tp"))
    return jax.shard_map(
        on_device,
        mesh=mesh,
        in_specs=placed,
        out_specs=(P("tp", "fsdp"), P("fsdp", "tp"), P(("tp", "fsdp"), None)),
        check_vma=False,
    )
```
